32 devices in a mesh: section: 4 (over y, core), expert: 4 (over z), mp: 2 (over x).
Axes of the slice: x: 2, y: 2, z: 4, core: 2. Of those that a mesh axis runs over, the one named last changes fastest.
Arguments:
- grad_top: bfloat16 [4, 64, 4096], P(None, 'expert', 'mp'), may hold values from -6 to 6
- w_down: bfloat16 [4, 4, 4096, 4096], P('section', 'expert', None, 'mp'), may hold values from -0.09375 to 0.09375
- w_up: bfloat16 [4, 4, 4096, 4096], P('section', 'expert', 'mp'), may hold values from -0.125 to 0.125
- saved: bfloat16 [4, 4, 4, 16, 4096], P('section', None, 'expert'), may hold values from -6 to 6
- assign: int32 [4, 4, 4, 4], P('section', None, 'expert'), may hold values from 0 to 3, as said below
- keep: int32 [4, 4], replicated, may hold values 0 or 1
Outputs:
- grads: bfloat16 [4, 4, 64, 4096], P('section', None, 'expert', 'mp')
The draws below stay inside these ranges and needn't reach their ends.
Inputs may be any that keep to these rules, and one draw needn't show every extreme that they name: Each row assign[l, m, i, :] names every expert exactly 1 times.
All inputs are finite; a program needn't handle non-finite values.
Results may differ from the reference program's by a relative error of at most 0.017.
Values may be sent and summed in bfloat16 or wider, within the bound.
A program may use at most 128 MiB of HBM per device.

```python
import jax
import jax.numpy as jnp
from jax import lax

D = 4096
FF = 4096
TILE = 4
PER = 1
MICRO = 4
SECTIONS = 4
EXPERTS = 4
GROUP = 1
FF_PART = 4096
TILES = 4
TOKENS = 64
ROWS_E = 16
N_EXPERT = 4


def draw_assign(key, part):
    count = SECTIONS * MICRO * N_EXPERT
    keys = jax.random.split(key, count)

    def draw_row(row_key):
        return jax.random.permutation(row_key, TILES)
    token_row_block = jax.vmap(draw_row)(keys)
    return (token_row_block // PER).reshape(SECTIONS, MICRO, N_EXPERT, TILES).astype(jnp.int32)


def plant(drawn, rng, low, high):
    longest = drawn.shape.index(max(drawn.shape))
    spots = []
    for shift in (0, 1):
        where = [jax.random.randint(jax.random.fold_in(rng, axis), (), 0, length) for axis, length in enumerate(drawn.shape)]
        where[longest] = (where[longest] + shift) % drawn.shape[longest]
        spots.append(tuple(where))
    return drawn.at[spots[0]].set(low).at[spots[1]].set(high)


def shard_levels(rng, shape, cuts, least, largest):
    loudness, own = 1.0, jax.random.fold_in(rng, 6)
    for axis_at, blocks in cuts:
        heights = jnp.exp(jax.random.uniform(jax.random.fold_in(own, axis_at), (blocks,), jnp.float32, least / len(cuts), largest / len(cuts)))
        loudness = loudness * jnp.repeat(heights, shape[axis_at] // blocks).reshape([-1 if axis == axis_at else 1 for axis in range(len(shape))])
    return loudness


def noise(stream_key, extent, deviation, bound, pieces=(), kind=jnp.bfloat16):
    loudness = shard_levels(stream_key, extent, pieces, -0.22, 0.18) if pieces else 1.0
    array = jax.random.normal(stream_key, extent, jnp.float32) * deviation * loudness
    return jnp.minimum(jnp.maximum(array, -bound), bound).astype(kind)


def setup_inputs(seed: int = 0) -> dict:
    key_list = jax.random.split(jax.random.key(seed), 7)
    grad_top = noise(key_list[0], (MICRO, TOKENS, D), 1.0, 6.0, ((1, 4), (2, 2)))
    w_down = noise(key_list[1], (SECTIONS, N_EXPERT, FF_PART, D), D ** -0.5, 0.09375, ((0, 4), (1, 4), (3, 2)))
    w_up = noise(key_list[2], (SECTIONS, N_EXPERT, D, FF_PART), (FF // 2) ** -0.5, 0.125, ((0, 4), (1, 4), (2, 2)))
    saved = noise(key_list[3], (SECTIONS, MICRO, N_EXPERT, ROWS_E, FF_PART), 1.0, 6.0, ((0, 4), (2, 4)))
    assign = draw_assign(jax.random.fold_in(key_list[6], 71), 0)
    keep = plant((jax.random.randint(key_list[5], (SECTIONS, MICRO), 0, 4) < 3).astype(jnp.int32), jax.random.fold_in(key_list[5], 1), 0, 1)
    return dict(grad_top=grad_top, w_down=w_down, w_up=w_up, saved=saved, assign=assign, keep=keep)


def apply_layer(current, down_all, up_all, stored, route_rows, factor):
    tiles = current.reshape(N_EXPERT, TILES, TILE, D)
    onehot = (route_rows[..., None] == jnp.arange(EXPERTS, dtype=jnp.int32)).astype(jnp.int32)
    before = jnp.cumsum(onehot, axis=1) - onehot
    tile_rank = jnp.sum(before * onehot, axis=-1).astype(jnp.int32)
    source = jnp.broadcast_to(jnp.arange(N_EXPERT, dtype=jnp.int32)[:, None], route_rows.shape)
    arrived = jnp.zeros((EXPERTS, N_EXPERT, PER, TILE, D), jnp.bfloat16).at[route_rows, source, tile_rank].set(tiles)

    def expert_step(expert_id):
        token_row_block = arrived[expert_id].reshape(ROWS_E, D)
        start = (expert_id * GROUP).astype(jnp.int32)
        down_weight_matrix = lax.dynamic_slice_in_dim(down_all, start, GROUP, 0)
        weights_up = lax.dynamic_slice_in_dim(up_all, start, GROUP, 0)
        pre_act = lax.dynamic_slice_in_dim(stored, start, GROUP, 0)
        hidden_state = jnp.einsum('ek,ytk->yet', token_row_block.astype(jnp.float32), down_weight_matrix.astype(jnp.float32))
        hidden_grad = jnp.where(pre_act > 0, hidden_state, 0.0).astype(jnp.bfloat16)
        parts = jnp.einsum('grf,gcf->grc', hidden_grad.astype(jnp.float32), weights_up.astype(jnp.float32)).astype(jnp.bfloat16)
        return jnp.sum(parts.astype(jnp.float32), axis=0)

    back_all = lax.map(expert_step, jnp.arange(EXPERTS, dtype=jnp.int32))
    back_all = back_all.reshape(EXPERTS, N_EXPERT, PER, TILE, D)
    row_updates = back_all[route_rows, source, tile_rank].reshape(TOKENS, D)
    return (current.astype(jnp.float32) + factor * row_updates).astype(jnp.bfloat16)


def reference(grad_top, w_down, w_up, saved, assign, keep):
    results = [[None for micro_index in range(MICRO)] for layer_index in range(SECTIONS)]
    for micro_index in range(MICRO):
        current = grad_top[micro_index]
        for layer_index in reversed(range(SECTIONS)):
            factor = keep[layer_index, micro_index].astype(jnp.float32)
            current = apply_layer(current, w_down[layer_index], w_up[layer_index], saved[layer_index, micro_index], assign[layer_index, micro_index], factor)
            results[layer_index][micro_index] = current
    return jnp.stack([jnp.stack(row_list) for row_list in results])
```

```python
import functools

import jax
import jax.numpy as jnp
from jax import lax
from jax.experimental import pallas as pl
from jax.experimental.pallas import tpu as pltpu
from jax.sharding import PartitionSpec as P

PER = 1
COL_CHUNKS = 2
FF_CHUNKS = 8
MESH = pl.DeviceIdType.MESH


def shifted(value, axis, by):
    peers = lax.axis_size(axis)
    pairs = [(i, i + by) for i in range(peers) if 0 <= i + by < peers]
    return lax.ppermute(value, axis, pairs)


def looped_body(grad_top, w_down, w_up, saved, assign, keep):
    n_section = lax.axis_size("section")
    n_expert = lax.axis_size("expert")
    section_index = lax.axis_index("section")
    tiles_dev = assign.shape[-1]
    experts = tiles_dev // PER
    group_size = n_expert // experts
    micro_count = grad_top.shape[0]
    token_rows = grad_top.shape[1]
    width = grad_top.shape[2]
    tile_rows = token_rows // tiles_dev
    slab_rows = PER * tile_rows
    down_projection = w_down[0, 0]
    up_proj = w_up[0, 0]
    stored = saved[0, :, 0]
    routes = assign[0, :, 0]
    rows_e = stored.shape[1]
    results = jnp.zeros((micro_count, token_rows, width), jnp.bfloat16)
    incoming = jnp.zeros((token_rows, width), jnp.bfloat16)
    steps_total = micro_count + n_section - 1
    for turn in range(steps_total):
        raw_index = turn - (n_section - 1) + section_index
        active = (raw_index >= 0) & (raw_index < micro_count)
        micro_index = jnp.clip(raw_index, 0, micro_count - 1)
        top_grad = lax.dynamic_index_in_dim(grad_top, micro_index, 0, keepdims=False)
        current = jnp.where(section_index == n_section - 1, top_grad, incoming)
        route_row = lax.dynamic_index_in_dim(routes, micro_index, 0, keepdims=False)
        onehot = (route_row[:, None] == jnp.arange(experts, dtype=jnp.int32)[None, :]).astype(
            jnp.int32
        )
        before = jnp.cumsum(onehot, axis=0) - onehot
        tile_rank = jnp.sum(before * onehot, axis=1)
        position_index = route_row * PER + tile_rank
        placing = (
            position_index[None, :] == jnp.arange(tiles_dev, dtype=jnp.int32)[:, None]
        ).astype(jnp.bfloat16)
        ordered = jnp.dot(
            placing,
            current.reshape(tiles_dev, tile_rows * width),
            preferred_element_type=jnp.float32,
        ).astype(jnp.bfloat16)
        outgoing = jnp.broadcast_to(
            ordered.reshape(experts, 1, slab_rows, width), (experts, group_size, slab_rows, width)
        )
        outgoing = outgoing.reshape(n_expert, slab_rows, width)
        arrived = lax.all_to_all(
            outgoing, "expert", split_axis=0, concat_axis=0, tiled=True
        ).reshape(rows_e, width)
        partial_value = lax.dot_general(
            arrived, down_projection, (((1,), (1,)), ((), ())), preferred_element_type=jnp.float32
        )
        pre_act = lax.dynamic_index_in_dim(stored, micro_index, 0, keepdims=False)
        expert_share_total = lax.psum_scatter(
            partial_value.astype(jnp.bfloat16), "mp", scatter_dimension=0, tiled=True
        ).astype(jnp.float32)
        share_rows = rows_e // lax.axis_size("mp")
        own_rows = lax.dynamic_slice_in_dim(
            pre_act, lax.axis_index("mp") * share_rows, share_rows, 0
        )
        local_grad = jnp.where(own_rows > 0, expert_share_total, 0.0).astype(jnp.bfloat16)
        hidden_grad = lax.all_gather(local_grad, "mp", axis=0, tiled=True)
        back_part = lax.dot_general(
            hidden_grad, up_proj, (((1,), (1,)), ((), ())), preferred_element_type=jnp.float32
        ).astype(jnp.bfloat16)
        returned = lax.all_to_all(
            back_part.reshape(n_expert, slab_rows, width),
            "expert",
            split_axis=0,
            concat_axis=0,
            tiled=True,
        )
        summed = jnp.sum(
            returned.reshape(experts, group_size, slab_rows, width), axis=1, dtype=jnp.float32
        )
        row_updates = jnp.take(summed, position_index, axis=0).reshape(token_rows, width)
        factor = keep[section_index, micro_index].astype(jnp.float32)
        fresh_grad = (current.astype(jnp.float32) + factor * row_updates).astype(jnp.bfloat16)
        previous = lax.dynamic_index_in_dim(results, micro_index, 0, keepdims=False)
        results = lax.dynamic_update_index_in_dim(
            results, jnp.where(active, fresh_grad, previous), micro_index, 0
        )
        if turn + 1 < steps_total:
            incoming = shifted(fresh_grad, "section", -1)
    return results[None]


NT = (((1,), (1,)), ((), ()))


def dot(a, b, dims=(((1,), (0,)), ((), ()))):
    return lax.dot_general(a, b, dims, preferred_element_type=jnp.float32)


def log2(n):
    return n.bit_length() - 1


def fused_kernel(
    n_section, n_expert, micro, tile,
    grad, stored, assign, keep, down_hbm, up_hbm,
    out,
    down, up, place, place_next, unplace, route, mask,
    ordered, arrived, partial, to_mate, from_mate, hidden_grad, back, fresh, handed, home,
    down_sem, up_sem, place_sems, out_sems, in_sems, mate_send, mate_recv,
    pass_send, pass_recv, home_send, home_recv,
):
    s = lax.axis_index("section")
    e = lax.axis_index("expert")
    x = lax.axis_index("mp")
    slab = micro * tile
    rows = n_expert * slab
    nc, _, cols = arrived.shape
    nf, _, fcols = partial.shape
    halves, _, fhalf = hidden_grad.shape
    f_per_half = nf // halves
    last = n_section - 1

    def block(i):
        return pl.ds(pl.multiple_of(i * slab, slab), slab)

    def down_copy(k, f):
        spot = pl.ds(pl.multiple_of(f * fcols, fcols), fcols)
        return pltpu.make_async_copy(
            down_hbm.at[0, 0, spot, pl.ds(k * cols, cols)], down.at[k, spot], down_sem.at[k, f]
        )

    def up_copy(h, k):
        spot = pl.ds(k * cols, cols)
        return pltpu.make_async_copy(
            up_hbm.at[0, 0, spot, pl.ds(h * fhalf, fhalf)], up.at[h, spot], up_sem.at[h, k]
        )

    for k in range(nc):
        for f in range(nf):
            down_copy(k, f).start()
    for h in range(halves):
        for k in range(nc):
            up_copy(h, k).start()

    above = lax.rem(s + 1, n_section)
    below = lax.rem(s + n_section - 1, n_section)
    barrier = pltpu.get_barrier_semaphore()
    pl.semaphore_signal(barrier, inc=1, device_id=(s, e, 1 - x), device_id_type=MESH)
    for d in range(n_expert):
        peer = lax.rem(e + d, n_expert)
        if d:
            pl.semaphore_signal(barrier, inc=1, device_id=(s, peer, x), device_id_type=MESH)
        pl.semaphore_signal(barrier, inc=1, device_id=(above, peer, x), device_id_type=MESH)
        pl.semaphore_signal(barrier, inc=1, device_id=(below, peer, x), device_id_type=MESH)

    def parts(index):
        return index >> log2(slab), (index >> log2(tile)) & (micro - 1), index & (tile - 1)

    def token_parts(index):
        return index >> log2(n_expert * tile), (index >> log2(tile)) & (n_expert - 1), index & (tile - 1)

    def placing(shape, token_axis):
        er, mr, rr = parts(lax.broadcasted_iota(jnp.int32, shape, 1 - token_axis))
        mt, tt, rt = token_parts(lax.broadcasted_iota(jnp.int32, shape, token_axis))
        chosen = jnp.zeros(shape, jnp.int32)
        for m in range(micro):
            for t in range(n_expert):
                chosen = jnp.where((mt == m) & (tt == t), assign[0, m, 0, t], chosen)
        hit = (chosen == er) & (mt == mr) & (rt == rr)
        return jnp.where(hit, 1.0, 0.0).astype(jnp.bfloat16)

    wide = place.shape
    place[...] = placing(wide, 1)
    unplace[...] = placing((rows, rows), 0)

    ir, mr, rr = parts(lax.broadcasted_iota(jnp.int32, (rows, rows), 0))
    mt, it, rt = token_parts(lax.broadcasted_iota(jnp.int32, (rows, rows), 1))
    swap = jnp.where((ir == it) & (mr == mt) & (rr == rt), 1.0, 0.0).astype(jnp.bfloat16)
    for f in range(nf):
        positive = jnp.where(
            stored[:, f * fcols : (f + 1) * fcols].astype(jnp.float32) > 0, 1.0, 0.0
        ).astype(jnp.bfloat16)
        mask[f] = dot(swap, positive).astype(jnp.bfloat16)

    _, row_micro, _ = parts(lax.broadcasted_iota(jnp.int32, (rows, cols), 0))
    factor = jnp.zeros((rows, cols), jnp.float32)
    for m in range(micro):
        factor = jnp.where(row_micro == m, keep[s, m].astype(jnp.float32), factor)

    pl.semaphore_wait(barrier, 3 * n_expert)

    def place_copy():
        return pltpu.make_async_remote_copy(
            place, place_next, place_sems.at[0], place_sems.at[1],
            device_id=(below, e, x), device_id_type=MESH,
        )

    @pl.when(s > 0)
    def _():
        place_copy().start()

    def dispatch_copy(k, d, receiving):
        peer = lax.rem(e + d, n_expert)
        slot = peer if receiving else e
        return pltpu.make_async_remote_copy(
            ordered.at[k, block(peer)], arrived.at[k, block(slot)],
            out_sems.at[k, d], in_sems.at[k, slot],
            device_id=(s, peer, x), device_id_type=MESH,
        )

    def pass_copy(k, d, receiving):
        peer = lax.rem(e + d, n_expert)
        slot = peer if receiving else e
        return pltpu.make_async_remote_copy(
            fresh.at[k, block(peer)], handed.at[k, block(slot)],
            pass_send.at[k, d], pass_recv.at[k, slot],
            device_id=(below, peer, x), device_id_type=MESH,
        )

    def home_copy(k, d, receiving):
        peer = lax.rem(e + d, n_expert)
        slot = peer if receiving else e
        return pltpu.make_async_remote_copy(
            fresh.at[k, block(peer)], home.at[k, block(slot)],
            home_send.at[k, d], home_recv.at[k, slot],
            device_id=(s, peer, x), device_id_type=MESH,
        )

    def mate_copy(f):
        return pltpu.make_async_remote_copy(
            to_mate.at[f], from_mate.at[f], mate_send.at[f], mate_recv.at[f],
            device_id=(s, e, 1 - x), device_id_type=MESH,
        )

    @pl.when(s < last)
    def _():
        place_copy().wait_recv()
        route[...] = dot(place[...], place_next[...], NT).astype(jnp.bfloat16)

    for k in range(nc):
        @pl.when(s == last)
        def _():
            ordered[k] = dot(
                place[:, :rows], grad[:, k * cols : (k + 1) * cols]
            ).astype(jnp.bfloat16)

        @pl.when(s < last)
        def _():
            for d in range(n_expert):
                pass_copy(k, d, True).wait_recv()
            ordered[k] = dot(route[...], handed[k]).astype(jnp.bfloat16)

        for d in range(1, n_expert):
            dispatch_copy(k, d, False).start()
        arrived[k, block(e)] = ordered[k, block(e)]

    for k in range(nc):
        for d in range(1, n_expert):
            dispatch_copy(k, d, True).wait_recv()

        @pl.loop(0, nf)
        def _(f):
            down_copy(k, f).wait()
            spot = pl.ds(pl.multiple_of(f * fcols, fcols), fcols)
            value = dot(arrived[k], down[k, spot], NT)
            if k:
                value = value + partial[f]
            partial[f] = value
            if k == nc - 1:
                to_mate[f] = value.astype(jnp.bfloat16)
                mate_copy(f).start()

    for h in range(halves):
        for q in range(f_per_half):
            f = h * f_per_half + q
            mate_copy(f).wait_recv()
            total = partial[f] + from_mate[f].astype(jnp.float32)
            hidden_grad[h, :, q * fcols : (q + 1) * fcols] = jnp.where(
                mask[f].astype(jnp.float32) > 0, total, 0.0
            ).astype(jnp.bfloat16)
        for k in range(nc):
            up_copy(h, k).wait()
            value = dot(hidden_grad[h], up[h, k * cols : (k + 1) * cols], NT)
            if h:
                value = value + back[k]
            if h < halves - 1:
                back[k] = value
            else:
                part = value.astype(jnp.bfloat16).astype(jnp.float32)
                fresh[k] = (arrived[k].astype(jnp.float32) + factor * part).astype(jnp.bfloat16)

                @pl.when(s > 0)
                def _():
                    for d in range(n_expert):
                        pass_copy(k, d, False).start()

                for d in range(1, n_expert):
                    home_copy(k, d, False).start()
                home[k, block(e)] = fresh[k, block(e)]

    for k in range(nc):
        for d in range(1, n_expert):
            home_copy(k, d, True).wait_recv()
        out[:, k * cols : (k + 1) * cols] = dot(unplace[...], home[k]).astype(jnp.bfloat16)

    for f in range(nf):
        mate_copy(f).wait_send()
    for k in range(nc):
        for d in range(1, n_expert):
            dispatch_copy(k, d, False).wait_send()
            home_copy(k, d, False).wait_send()

    @pl.when(s > 0)
    def _():
        place_copy().wait_send()
        for k in range(nc):
            for d in range(n_expert):
                pass_copy(k, d, False).wait_send()


def fused_body(mesh_shape, grad_top, w_down, w_up, saved, assign, keep):
    n_section, n_expert = mesh_shape["section"], mesh_shape["expert"]
    micro, token_rows, width = grad_top.shape
    hidden = w_down.shape[2]
    tile = token_rows // n_expert
    rows = micro * token_rows
    cols, fcols, halves = width // COL_CHUNKS, hidden // FF_CHUNKS, 2
    nc, nf = COL_CHUNKS, FF_CHUNKS
    bf16, f32 = jnp.bfloat16, jnp.float32
    dma = pltpu.SemaphoreType.DMA
    vmem = pl.BlockSpec(memory_space=pltpu.VMEM)
    smem = pl.BlockSpec(memory_space=pltpu.SMEM)
    anyspace = pl.BlockSpec(memory_space=pl.ANY)
    wide = max(rows, 128)
    result = pl.pallas_call(
        functools.partial(fused_kernel, n_section, n_expert, micro, tile),
        out_shape=jax.ShapeDtypeStruct((rows, width), bf16),
        in_specs=[vmem, vmem, smem, smem, anyspace, anyspace],
        out_specs=vmem,
        scratch_shapes=[
            pltpu.VMEM((nc, hidden, cols), bf16),
            pltpu.VMEM((halves, width, hidden // halves), bf16),
            pltpu.VMEM((rows, wide), bf16),
            pltpu.VMEM((rows, wide), bf16),
            pltpu.VMEM((rows, rows), bf16),
            pltpu.VMEM((rows, rows), bf16),
            pltpu.VMEM((nf, rows, fcols), bf16),
            pltpu.VMEM((nc, rows, cols), bf16),
            pltpu.VMEM((nc, rows, cols), bf16),
            pltpu.VMEM((nf, rows, fcols), f32),
            pltpu.VMEM((nf, rows, fcols), bf16),
            pltpu.VMEM((nf, rows, fcols), bf16),
            pltpu.VMEM((halves, rows, hidden // halves), bf16),
            pltpu.VMEM((nc, rows, cols), f32),
            pltpu.VMEM((nc, rows, cols), bf16),
            pltpu.VMEM((nc, rows, cols), bf16),
            pltpu.VMEM((nc, rows, cols), bf16),
            dma((nc, nf)),
            dma((halves, nc)),
            dma((2,)),
            dma((nc, n_expert)),
            dma((nc, n_expert)),
            dma((nf,)),
            dma((nf,)),
            dma((nc, n_expert)),
            dma((nc, n_expert)),
            dma((nc, n_expert)),
            dma((nc, n_expert)),
        ],
        compiler_params=pltpu.CompilerParams(
            collective_id=0, has_side_effects=True, vmem_limit_bytes=52 * 1024 * 1024
        ),
    )(
        grad_top.reshape(rows, width),
        saved.reshape(rows, hidden),
        assign,
        keep,
        w_down,
        w_up,
    )
    return result.reshape(1, micro, token_rows, width)


def power_of_two(n):
    return n & (n - 1) == 0


def body(mesh_shape, grad_top, w_down, w_up, saved, assign, keep):
    n_section, n_expert = mesh_shape["section"], mesh_shape["expert"]
    micro, token_rows, width = grad_top.shape
    hidden = w_down.shape[2]
    tiles = assign.shape[-1]
    weights = 2 * (w_down.size + w_up.size)
    fits = (
        PER == 1
        and tiles == n_expert
        and mesh_shape["mp"] == 2
        and n_section >= 3
        and power_of_two(micro)
        and power_of_two(n_expert)
        and power_of_two(token_rows // tiles)
        and (micro * token_rows // tiles) % 16 == 0
        and micro * token_rows <= 128
        and width % (128 * COL_CHUNKS) == 0
        and hidden % (128 * FF_CHUNKS) == 0
        and weights <= 33554432
    )
    chosen = functools.partial(fused_body, mesh_shape) if fits else looped_body
    return chosen(grad_top, w_down, w_up, saved, assign, keep)


def solution(mesh):
    placed = (
        P(None, "expert", "mp"),
        P("section", "expert", None, "mp"),
        P("section", "expert", "mp", None),
        P("section", None, "expert", None, None),
        P("section", None, "expert", None),
        P(),
    )
    return jax.shard_map(
        functools.partial(body, mesh.shape),
        mesh=mesh,
        in_specs=placed,
        out_specs=P("section", None, "expert", "mp"),
        check_vma=False,
    )
```

```python
import functools

import jax
import jax.numpy as jnp
from jax import lax
from jax.experimental import pallas as pl
from jax.experimental.pallas import tpu as pltpu
from jax.sharding import PartitionSpec as P

PER = 1
GROUPS = 1
COL_CHUNKS = 2
FF_CHUNKS = 8
FF_HALVES = 2
VMEM_BYTES = 63 * 1024 * 1024
MESH = pl.DeviceIdType.MESH


def shifted(value, axis, by):
    peers = lax.axis_size(axis)
    pairs = [(i, i + by) for i in range(peers) if 0 <= i + by < peers]
    return lax.ppermute(value, axis, pairs)


def looped_body(grad_top, w_down, w_up, saved, assign, keep):
    n_section = lax.axis_size("section")
    n_expert = lax.axis_size("expert")
    section_index = lax.axis_index("section")
    tiles_dev = assign.shape[-1]
    experts = tiles_dev // PER
    group_size = n_expert // experts
    micro_count = grad_top.shape[0]
    token_rows = grad_top.shape[1]
    width = grad_top.shape[2]
    tile_rows = token_rows // tiles_dev
    slab_rows = PER * tile_rows
    down_projection = w_down[0, 0]
    up_proj = w_up[0, 0]
    stored = saved[0, :, 0]
    routes = assign[0, :, 0]
    rows_e = stored.shape[1]
    results = jnp.zeros((micro_count, token_rows, width), jnp.bfloat16)
    incoming = jnp.zeros((token_rows, width), jnp.bfloat16)
    steps_total = micro_count + n_section - 1
    for turn in range(steps_total):
        raw_index = turn - (n_section - 1) + section_index
        active = (raw_index >= 0) & (raw_index < micro_count)
        micro_index = jnp.clip(raw_index, 0, micro_count - 1)
        top_grad = lax.dynamic_index_in_dim(grad_top, micro_index, 0, keepdims=False)
        current = jnp.where(section_index == n_section - 1, top_grad, incoming)
        route_row = lax.dynamic_index_in_dim(routes, micro_index, 0, keepdims=False)
        onehot = (route_row[:, None] == jnp.arange(experts, dtype=jnp.int32)[None, :]).astype(
            jnp.int32
        )
        before = jnp.cumsum(onehot, axis=0) - onehot
        tile_rank = jnp.sum(before * onehot, axis=1)
        position_index = route_row * PER + tile_rank
        placing = (
            position_index[None, :] == jnp.arange(tiles_dev, dtype=jnp.int32)[:, None]
        ).astype(jnp.bfloat16)
        ordered = jnp.dot(
            placing,
            current.reshape(tiles_dev, tile_rows * width),
            preferred_element_type=jnp.float32,
        ).astype(jnp.bfloat16)
        outgoing = jnp.broadcast_to(
            ordered.reshape(experts, 1, slab_rows, width), (experts, group_size, slab_rows, width)
        )
        outgoing = outgoing.reshape(n_expert, slab_rows, width)
        arrived = lax.all_to_all(
            outgoing, "expert", split_axis=0, concat_axis=0, tiled=True
        ).reshape(rows_e, width)
        partial_value = lax.dot_general(
            arrived, down_projection, (((1,), (1,)), ((), ())), preferred_element_type=jnp.float32
        )
        pre_act = lax.dynamic_index_in_dim(stored, micro_index, 0, keepdims=False)
        expert_share_total = lax.psum_scatter(
            partial_value.astype(jnp.bfloat16), "mp", scatter_dimension=0, tiled=True
        ).astype(jnp.float32)
        share_rows = rows_e // lax.axis_size("mp")
        own_rows = lax.dynamic_slice_in_dim(
            pre_act, lax.axis_index("mp") * share_rows, share_rows, 0
        )
        local_grad = jnp.where(own_rows > 0, expert_share_total, 0.0).astype(jnp.bfloat16)
        hidden_grad = lax.all_gather(local_grad, "mp", axis=0, tiled=True)
        back_part = lax.dot_general(
            hidden_grad, up_proj, (((1,), (1,)), ((), ())), preferred_element_type=jnp.float32
        ).astype(jnp.bfloat16)
        returned = lax.all_to_all(
            back_part.reshape(n_expert, slab_rows, width),
            "expert",
            split_axis=0,
            concat_axis=0,
            tiled=True,
        )
        summed = jnp.sum(
            returned.reshape(experts, group_size, slab_rows, width), axis=1, dtype=jnp.float32
        )
        row_updates = jnp.take(summed, position_index, axis=0).reshape(token_rows, width)
        factor = keep[section_index, micro_index].astype(jnp.float32)
        fresh_grad = (current.astype(jnp.float32) + factor * row_updates).astype(jnp.bfloat16)
        previous = lax.dynamic_index_in_dim(results, micro_index, 0, keepdims=False)
        results = lax.dynamic_update_index_in_dim(
            results, jnp.where(active, fresh_grad, previous), micro_index, 0
        )
        if turn + 1 < steps_total:
            incoming = shifted(fresh_grad, "section", -1)
    return results[None]


NT = (((1,), (1,)), ((), ()))


def dot(a, b, dims=(((1,), (0,)), ((), ()))):
    return lax.dot_general(a, b, dims, preferred_element_type=jnp.float32)


def log2(n):
    return n.bit_length() - 1


def fused_kernel(
    n_section, n_expert, micro, tile,
    grad_hbm, stored_hbm, assign_hbm, keep_hbm, down_hbm, up_hbm,
    out,
    grad, stored, assign, keep,
    down, up, place, place_next, unplace, route, mask,
    ordered, arrived, partial, to_mate, from_mate, hidden_grad, back, fresh, handed, home,
    load_sem, down_sem, up_sem, place_sems, out_sems, in_sems, mate_send, mate_recv,
    pass_send, pass_recv, home_send, home_recv, lift_sems,
):
    s = lax.axis_index("section")
    e = lax.axis_index("expert")
    x = lax.axis_index("mp")
    groups, nc, rows, cols = arrived.shape
    per = micro // groups
    slab = per * tile
    _, nf, _, fcols = partial.shape
    _, halves, _, fhalf = hidden_grad.shape
    f_per_half = nf // halves
    last = n_section - 1

    def block(i):
        return pl.ds(pl.multiple_of(i * slab, slab), slab)

    def loads():
        pairs = ((assign_hbm, assign), (keep_hbm, keep), (grad_hbm, grad), (stored_hbm, stored))
        return [
            pltpu.make_async_copy(source, spot, load_sem.at[i])
            for i, (source, spot) in enumerate(pairs)
        ]

    def down_copy(k, f):
        spot = pl.ds(pl.multiple_of(f * fcols, fcols), fcols)
        return pltpu.make_async_copy(
            down_hbm.at[0, 0, spot, pl.ds(k * cols, cols)], down.at[k, spot], down_sem.at[k, f]
        )

    def up_copy(h, k):
        spot = pl.ds(k * cols, cols)
        return pltpu.make_async_copy(
            up_hbm.at[0, 0, spot, pl.ds(h * fhalf, fhalf)], up.at[h, spot], up_sem.at[h, k]
        )

    above = lax.rem(s + 1, n_section)
    below = lax.rem(s + n_section - 1, n_section)
    barrier = pltpu.get_barrier_semaphore()
    pl.semaphore_signal(barrier, inc=1, device_id=(s, e, 1 - x), device_id_type=MESH)
    for d in range(n_expert):
        peer = lax.rem(e + d, n_expert)
        if d:
            pl.semaphore_signal(barrier, inc=1, device_id=(s, peer, x), device_id_type=MESH)
        pl.semaphore_signal(barrier, inc=1, device_id=(above, peer, x), device_id_type=MESH)
        pl.semaphore_signal(barrier, inc=1, device_id=(below, peer, x), device_id_type=MESH)

    for copy in loads():
        copy.start()
    for k in range(nc):
        for f in range(nf):
            down_copy(k, f).start()
    for h in range(halves):
        for k in range(nc):
            up_copy(h, k).start()

    def parts(index):
        return index >> log2(slab), (index >> log2(tile)) & (per - 1), index & (tile - 1)

    def token_parts(index):
        return index >> log2(n_expert * tile), (index >> log2(tile)) & (n_expert - 1), index & (tile - 1)

    def placing(g, shape, token_axis):
        er, mr, rr = parts(lax.broadcasted_iota(jnp.int32, shape, 1 - token_axis))
        mt, tt, rt = token_parts(lax.broadcasted_iota(jnp.int32, shape, token_axis))
        chosen = jnp.zeros(shape, jnp.int32)
        for m in range(per):
            for t in range(n_expert):
                chosen = jnp.where((mt == m) & (tt == t), assign[0, g * per + m, 0, t], chosen)
        hit = (chosen == er) & (mt == mr) & (rt == rr)
        return jnp.where(hit, 1.0, 0.0).astype(jnp.bfloat16)

    def place_copy():
        return pltpu.make_async_remote_copy(
            place, place_next, place_sems.at[0], place_sems.at[1],
            device_id=(below, e, x), device_id_type=MESH,
        )

    def dispatch_copy(g, k, d, receiving):
        peer = lax.rem(e + d, n_expert)
        if d == 0:
            return pltpu.make_async_copy(
                ordered.at[g, k, block(e)], arrived.at[g, k, block(e)], out_sems.at[g, k, 0]
            )
        slot = peer if receiving else e
        return pltpu.make_async_remote_copy(
            ordered.at[g, k, block(peer)], arrived.at[g, k, block(slot)],
            out_sems.at[g, k, d], in_sems.at[g, k, slot],
            device_id=(s, peer, x), device_id_type=MESH,
        )

    def pass_copy(g, k, d, receiving):
        peer = lax.rem(e + d, n_expert)
        slot = peer if receiving else e
        return pltpu.make_async_remote_copy(
            fresh.at[g, k, block(peer)], handed.at[g, k, block(slot)],
            pass_send.at[g, k, d], pass_recv.at[g, k, slot],
            device_id=(below, peer, x), device_id_type=MESH,
        )

    def home_copy(g, k, d, receiving):
        peer = lax.rem(e + d, n_expert)
        if d == 0:
            return pltpu.make_async_copy(
                fresh.at[g, k, block(e)], home.at[g, k, block(e)], home_send.at[g, k, 0]
            )
        slot = peer if receiving else e
        return pltpu.make_async_remote_copy(
            fresh.at[g, k, block(peer)], home.at[g, k, block(slot)],
            home_send.at[g, k, d], home_recv.at[g, k, slot],
            device_id=(s, peer, x), device_id_type=MESH,
        )

    def lift_copy(g, k):
        return pltpu.make_async_remote_copy(
            handed.at[g, k], home.at[g, k], lift_sems.at[0, g, k], lift_sems.at[1, g, k],
            device_id=(above, e, x), device_id_type=MESH,
        )

    def mate_copy(g, f):
        return pltpu.make_async_remote_copy(
            to_mate.at[g, f], from_mate.at[g, f], mate_send.at[g, f], mate_recv.at[g, f],
            device_id=(s, e, 1 - x), device_id_type=MESH,
        )

    assign_load, keep_load, grad_load, stored_load = loads()
    assign_load.wait()
    keep_load.wait()
    for g in range(groups):
        place[g] = placing(g, place.shape[1:], 1)
        unplace[g] = placing(g, (rows, rows), 0)

    pl.semaphore_wait(barrier, 3 * n_expert)

    @pl.when(s > 0)
    def _():
        place_copy().start()

    grad_load.wait()

    @pl.when(s == last)
    def _():
        for g in range(groups):
            for k in range(nc):
                ordered[g, k] = dot(
                    place[g, :, :rows],
                    grad[g * rows : (g + 1) * rows, k * cols : (k + 1) * cols],
                ).astype(jnp.bfloat16)
                for d in (*range(1, n_expert), 0):
                    dispatch_copy(g, k, d, False).start()

    ir, mr, rr = parts(lax.broadcasted_iota(jnp.int32, (rows, rows), 0))
    mt, it, rt = token_parts(lax.broadcasted_iota(jnp.int32, (rows, rows), 1))
    swap = jnp.where((ir == it) & (mr == mt) & (rr == rt), 1.0, 0.0).astype(jnp.bfloat16)
    stored_load.wait()
    for g in range(groups):
        for f in range(nf):
            block_stored = stored[g * rows : (g + 1) * rows, f * fcols : (f + 1) * fcols]
            positive = jnp.where(block_stored.astype(jnp.float32) > 0, 1.0, 0.0)
            mask[g, f] = dot(swap, positive.astype(jnp.bfloat16)).astype(jnp.bfloat16)

    _, row_micro, _ = parts(lax.broadcasted_iota(jnp.int32, (rows, cols), 0))

    @pl.when(s < last)
    def _():
        place_copy().wait_recv()
        for g in range(groups):
            route[g] = dot(place[g], place_next[g], NT).astype(jnp.bfloat16)

    def enter(g):
        @pl.when(s < last)
        def _():
            for k in range(nc):
                for d in range(n_expert):
                    pass_copy(g, k, d, True).wait_recv()
                ordered[g, k] = dot(route[g], handed[g, k]).astype(jnp.bfloat16)
                for d in (*range(1, n_expert), 0):
                    dispatch_copy(g, k, d, False).start()

        for k in range(nc):
            dispatch_copy(g, k, 0, False).wait()
            for d in range(1, n_expert):
                dispatch_copy(g, k, d, True).wait_recv()
            for f in range(nf):
                if g == 0:
                    down_copy(k, f).wait()
                value = dot(arrived[g, k], down[k, f * fcols : (f + 1) * fcols], NT)
                if k:
                    value = value + partial[g, f]
                partial[g, f] = value
                if k == nc - 1:
                    to_mate[g, f] = value.astype(jnp.bfloat16)
                    mate_copy(g, f).start()

        @pl.when(s < last)
        def _():
            for k in range(nc):
                lift_copy(g, k).start()

    def leave(g):
        factor = jnp.zeros((rows, cols), jnp.float32)
        for m in range(per):
            factor = jnp.where(row_micro == m, keep[s, g * per + m].astype(jnp.float32), factor)
        for h in range(halves):
            for q in range(f_per_half):
                f = h * f_per_half + q
                mate_copy(g, f).wait_recv()
                total = partial[g, f] + from_mate[g, f].astype(jnp.float32)
                hidden_grad[g, h, :, q * fcols : (q + 1) * fcols] = jnp.where(
                    mask[g, f].astype(jnp.float32) > 0, total, 0.0
                ).astype(jnp.bfloat16)
            for k in range(nc):
                if g == 0:
                    up_copy(h, k).wait()
                value = dot(hidden_grad[g, h], up[h, k * cols : (k + 1) * cols], NT)
                if h:
                    value = value + back[g, k]
                if h < halves - 1:
                    back[g, k] = value
                else:
                    part = value.astype(jnp.bfloat16).astype(jnp.float32)
                    fresh[g, k] = (arrived[g, k].astype(jnp.float32) + factor * part).astype(
                        jnp.bfloat16
                    )

                    @pl.when(s > 0)
                    def _():
                        for d in range(n_expert):
                            pass_copy(g, k, d, False).start()

                    @pl.when(s == 0)
                    def _():
                        for d in (*range(1, n_expert), 0):
                            home_copy(g, k, d, False).start()

    for g in range(groups):
        enter(g)
        leave(g)

    for g in range(groups):
        for k in range(nc):
            @pl.when(s == 0)
            def _():
                home_copy(g, k, 0, False).wait()
                for d in range(1, n_expert):
                    home_copy(g, k, d, True).wait_recv()

            @pl.when(s > 0)
            def _():
                lift_copy(g, k).wait_recv()

            out[g * rows : (g + 1) * rows, k * cols : (k + 1) * cols] = dot(
                unplace[g], home[g, k]
            ).astype(jnp.bfloat16)

    for g in range(groups):
        for f in range(nf):
            mate_copy(g, f).wait_send()
        for k in range(nc):
            for d in range(1, n_expert):
                dispatch_copy(g, k, d, False).wait_send()

            @pl.when(s == 0)
            def _():
                for d in range(1, n_expert):
                    home_copy(g, k, d, False).wait_send()

            @pl.when(s > 0)
            def _():
                for d in range(n_expert):
                    pass_copy(g, k, d, False).wait_send()

            @pl.when(s < last)
            def _():
                lift_copy(g, k).wait_send()

    @pl.when(s > 0)
    def _():
        place_copy().wait_send()


def fused_body(mesh_shape, grad_top, w_down, w_up, saved, assign, keep):
    n_section, n_expert = mesh_shape["section"], mesh_shape["expert"]
    micro, token_rows, width = grad_top.shape
    hidden = w_down.shape[2]
    tile = token_rows // n_expert
    groups, nc, nf, halves = GROUPS, COL_CHUNKS, FF_CHUNKS, FF_HALVES
    total_rows = micro * token_rows
    rows = total_rows // groups
    cols, fcols, fhalf = width // nc, hidden // nf, hidden // halves
    bf16, f32 = jnp.bfloat16, jnp.float32
    dma = pltpu.SemaphoreType.DMA
    anyspace = pl.BlockSpec(memory_space=pl.ANY)
    wide = max(rows, 128)
    by_column = (groups, nc, rows, cols)
    by_hidden = (groups, nf, rows, fcols)
    result = pl.pallas_call(
        functools.partial(fused_kernel, n_section, n_expert, micro, tile),
        out_shape=jax.ShapeDtypeStruct((total_rows, width), bf16),
        in_specs=[anyspace] * 6,
        out_specs=pl.BlockSpec(memory_space=pltpu.VMEM),
        scratch_shapes=[
            pltpu.VMEM((total_rows, width), bf16),
            pltpu.VMEM((total_rows, hidden), bf16),
            pltpu.SMEM(assign.shape, jnp.int32),
            pltpu.SMEM(keep.shape, jnp.int32),
            pltpu.VMEM((nc, hidden, cols), bf16),
            pltpu.VMEM((halves, width, fhalf), bf16),
            pltpu.VMEM((groups, rows, wide), bf16),
            pltpu.VMEM((groups, rows, wide), bf16),
            pltpu.VMEM((groups, rows, rows), bf16),
            pltpu.VMEM((groups, rows, rows), bf16),
            pltpu.VMEM(by_hidden, bf16),
            pltpu.VMEM(by_column, bf16),
            pltpu.VMEM(by_column, bf16),
            pltpu.VMEM(by_hidden, f32),
            pltpu.VMEM(by_hidden, bf16),
            pltpu.VMEM(by_hidden, bf16),
            pltpu.VMEM((groups, halves, rows, fhalf), bf16),
            pltpu.VMEM(by_column, f32),
            pltpu.VMEM(by_column, bf16),
            pltpu.VMEM(by_column, bf16),
            pltpu.VMEM(by_column, bf16),
            dma((4,)),
            dma((nc, nf)),
            dma((halves, nc)),
            dma((2,)),
            dma((groups, nc, n_expert)),
            dma((groups, nc, n_expert)),
            dma((groups, nf)),
            dma((groups, nf)),
            dma((groups, nc, n_expert)),
            dma((groups, nc, n_expert)),
            dma((groups, nc, n_expert)),
            dma((groups, nc, n_expert)),
            dma((2, groups, nc)),
        ],
        compiler_params=pltpu.CompilerParams(
            collective_id=0, has_side_effects=True, vmem_limit_bytes=VMEM_BYTES
        ),
    )(
        grad_top.reshape(total_rows, width),
        saved.reshape(total_rows, hidden),
        assign,
        keep,
        w_down,
        w_up,
    )
    return result.reshape(1, micro, token_rows, width)


def power_of_two(n):
    return n & (n - 1) == 0


def body(mesh_shape, grad_top, w_down, w_up, saved, assign, keep):
    n_section, n_expert = mesh_shape["section"], mesh_shape["expert"]
    micro, token_rows, width = grad_top.shape
    hidden = w_down.shape[2]
    tiles = assign.shape[-1]
    weights = 2 * (w_down.size + w_up.size)
    fits = (
        PER == 1
        and tiles == n_expert
        and mesh_shape["mp"] == 2
        and n_section >= 3
        and power_of_two(micro)
        and micro % GROUPS == 0
        and power_of_two(n_expert)
        and power_of_two(token_rows // tiles)
        and (micro * token_rows // tiles) % (8 * GROUPS) == 0
        and micro * token_rows <= 128
        and width % (128 * COL_CHUNKS) == 0
        and hidden % (128 * FF_CHUNKS) == 0
        and weights <= 33554432
    )
    chosen = functools.partial(fused_body, mesh_shape) if fits else looped_body
    return chosen(grad_top, w_down, w_up, saved, assign, keep)


def solution(mesh):
    placed = (
        P(None, "expert", "mp"),
        P("section", "expert", None, "mp"),
        P("section", "expert", "mp", None),
        P("section", None, "expert", None, None),
        P("section", None, "expert", None),
        P(),
    )
    return jax.shard_map(
        functools.partial(body, mesh.shape),
        mesh=mesh,
        in_specs=placed,
        out_specs=P("section", None, "expert", "mp"),
        check_vma=False,
    )
```
